32 devices in a mesh: sec: 8 (over y, x, core), op: 4 (over z).
Axes of the slice: x: 2, y: 2, z: 4, core: 2. Of those that a mesh axis runs over, the one named last changes fastest.
Arguments:
- psi: bfloat16 [8, 512, 512], P('sec', 'op'), may hold values from -6 to 6
- left_ops: bfloat16 [24, 8, 512, 512], P(None, 'sec', None, 'op'), may hold values from -0.0546875 to 0.0546875
- right_ops: bfloat16 [24, 8, 512, 512], P(None, 'sec', 'op'), may hold values from -0.25 to 0.25
- sources: int32 [8, 24], P('sec'), may hold values from 0 to 7
- counts: int32 [8], P('sec'), may hold values from 6 to 24, as said below
- dims_left: int32 [8], P('sec'), may hold values from 128 to 512, as said below
- dims_right: int32 [8], P('sec'), may hold values from 128 to 512, as said below
Outputs:
- sigma: bfloat16 [8, 512, 512], P('sec', 'op')
The draws below stay inside these ranges and needn't reach their ends.
Inputs may be any that keep to these rules, and one draw needn't show every extreme that they name: `counts`: some sector has all 24 terms active. `dims_left`: some sector has the full padded dimension. `dims_right`: some sector has the full padded dimension.
All inputs are finite; a program needn't handle non-finite values.
Results may differ from the reference program's by a relative error of at most 0.0049.
Values may be sent and summed in bfloat16 or wider, within the bound.
A program may use at most 128 MiB of HBM per device.

```python
import jax
import jax.numpy as jnp
from jax import lax

BLK = 512
K = 24
S = 8


def forced_draw(key, low, high):
    first_key, second_key = jax.random.split(key)
    drawn = jax.random.randint(first_key, (S,), low, high + 1)
    location = jax.random.randint(second_key, (), 0, S)
    return drawn.at[location].set(high).astype(jnp.int32)


def draw_counts(key, part):
    return forced_draw(jax.random.fold_in(key, 11), max(K // 4, 1), K)


def draw_dims_left(key, part):
    return forced_draw(jax.random.fold_in(key, 23), BLK // 4, BLK)


def draw_dims_right(key, part):
    return forced_draw(jax.random.fold_in(key, 37), BLK // 4, BLK)


def place_ends(values, stream_key, low, top_value):
    longest = values.shape.index(max(values.shape))
    spots = []
    for shift in (0, 1):
        where = [jax.random.randint(jax.random.fold_in(stream_key, axis), (), 0, length) for axis, length in enumerate(values.shape)]
        where[longest] = (where[longest] + shift) % values.shape[longest]
        spots.append(tuple(where))
    return values.at[spots[0]].set(low).at[spots[1]].set(top_value)


def block_levels(own_key, extent, cuts, least, top_value):
    def one(axis_at, parts):
        draws = jax.random.uniform(jax.random.fold_in(jax.random.fold_in(own_key, 6), axis_at), (parts,), jnp.float32, least / len(cuts), top_value / len(cuts))
        return jnp.repeat(jnp.exp(draws), extent[axis_at] // parts).reshape((-1,) + (1,) * (len(extent) - axis_at - 1))

    level = one(*cuts[0])
    for cut in cuts[1:]:
        level = level * one(*cut)
    return level


def normal_values(own_key, dims, scale, most, shards=(), held_as=jnp.bfloat16):
    values = scale * jax.random.normal(own_key, dims, jnp.float32)
    if shards:
        values = values * block_levels(own_key, dims, shards, -0.22, 0.18)
    return jnp.clip(values, -most, most).astype(held_as)


def setup_inputs(seed: int = 0) -> dict:
    keys = jax.random.split(jax.random.key(seed), 8)
    psi = normal_values(keys[0], (S, BLK, BLK), 1.0, 6.0, ((0, 8), (1, 4)))
    left_ops = normal_values(keys[1], (K, S, BLK, BLK), (BLK * K) ** -0.5, 0.0546875, ((1, 8), (3, 4)))
    right_ops = normal_values(keys[2], (K, S, BLK, BLK), BLK ** -0.5, 0.25, ((1, 8), (2, 4)))
    sources = place_ends(jax.random.randint(keys[3], (S, K), 0, S), jax.random.fold_in(keys[3], 1), 0, S - 1).astype(jnp.int32)
    counts = draw_counts(jax.random.fold_in(keys[7], 71), 0)
    dims_left = draw_dims_left(jax.random.fold_in(keys[7], 71), 0)
    dims_right = draw_dims_right(jax.random.fold_in(keys[7], 71), 0)
    return dict(psi=psi, left_ops=left_ops, right_ops=right_ops, sources=sources, counts=counts, dims_left=dims_left, dims_right=dims_right)


def reference(psi, left_ops, right_ops, sources, counts, dims_left, dims_right):
    row_ids = lax.broadcasted_iota(jnp.int32, (S, BLK, BLK), 1)
    col_ids = lax.broadcasted_iota(jnp.int32, (S, BLK, BLK), 2)
    inside_mask = (row_ids < dims_left[:, None, None]) & (col_ids < dims_right[:, None, None])
    panel = jnp.where(inside_mask, psi, jnp.zeros_like(psi))

    def one_sector(sector):
        chosen = jnp.take(panel, sources[sector], axis=0)
        right_blocks = right_ops[:, sector]
        image = jnp.einsum("kab,kcb->kac", chosen.astype(jnp.float32), right_blocks.astype(jnp.float32))
        image = image.astype(jnp.bfloat16)
        active = jnp.arange(K, dtype=jnp.int32) < counts[sector]
        image = jnp.where(active[:, None, None], image, jnp.zeros_like(image))
        summed = jnp.einsum("kab,kbc->ac", left_ops[:, sector].astype(jnp.float32), image.astype(jnp.float32))
        summed = jnp.where(inside_mask[sector], summed, jnp.zeros_like(summed))
        return summed.astype(jnp.bfloat16)

    return lax.map(one_sector, jnp.arange(S, dtype=jnp.int32))
```

```python
import functools

import jax
import jax.numpy as jnp
from jax import lax
from jax.experimental import pallas as pl
from jax.experimental.pallas import tpu as pltpu
from jax.sharding import PartitionSpec as P

MESH = pl.DeviceIdType.MESH


def flip(j, q):
    out, bit = 0, 1
    while bit <= q:
        out = out + ((j // bit + q // bit % 2) % 2) * bit
        bit *= 2
    return out + j // bit * bit


def kernel(n_sec, n_op, chunks, parts, psi_hbm, left_hbm, right_hbm, src_ref, cnt_ref, dl_ref, dr_ref, out_ref,
           *scratch):
    pan, at = [], 0
    for q in range(n_op):
        pan.append(scratch[at:at + len(parts[q])])
        at += len(parts[q])
    (psi_v, lv, rv, xs, xr, acc, local_sem, z_send, z_recv, s_send, s_recv, m_send, m_recv, x_send, x_recv,
     near_out, near_in, far_out, far_in, near_send, near_recv, far_send, far_recv) = scratch[at:]
    s = lax.axis_index("sec")
    j = lax.axis_index("op")
    groups = n_sec // 2
    g, core = s // 2, s % 2
    mate = g * 2 + 1 - core
    rows, cols = psi_v.shape
    terms = lv.shape[0]
    width = rv.shape[1]
    per = terms // chunks
    high = n_op // 2
    order = [high] + list(range(1, high)) + list(range(high + 1, n_op))
    early, late = ((1, 2), (0, 3)) if n_op == 4 else ((), tuple(range(n_op)))

    load_p = pltpu.make_async_copy(psi_hbm, psi_v, local_sem.at[2])
    load_r = pltpu.make_async_copy(right_hbm, rv, local_sem.at[0])
    load_l = pltpu.make_async_copy(left_hbm, lv, local_sem.at[1])

    def op_at(q):
        return flip(j, q)

    def from_group(d):
        return (g - d + groups) % groups

    barrier = pltpu.get_barrier_semaphore()
    for q in range(1, n_op):
        pl.semaphore_signal(barrier, inc=1, device_id={"op": op_at(q)}, device_id_type=MESH)

    @pl.loop(1, groups)
    def _(d):
        pl.semaphore_signal(barrier, inc=1, device_id={"sec": ((g + d) % groups) * 2 + core}, device_id_type=MESH)

    pl.semaphore_signal(barrier, inc=1, device_id={"sec": mate}, device_id_type=MESH)

    load_p.start()
    load_r.start()
    load_l.start()

    def inside():
        row_ids = j * rows + lax.broadcasted_iota(jnp.int32, (rows, cols), 0)
        col_ids = lax.broadcasted_iota(jnp.int32, (rows, cols), 1)
        return (row_ids < dl_ref[0, 0]) & (col_ids < dr_ref[0, 0])

    keep = inside()
    acc[...] = jnp.zeros_like(acc)
    load_p.wait()
    psi = psi_v[...]
    pan[0][0][s] = jnp.where(keep, psi, jnp.zeros_like(psi))

    pl.semaphore_wait(barrier, n_op - 1 + groups)

    def part_of(h, q):
        return pl.ds(sum(parts[q][:h]), parts[q][h])

    def z_copy(q, h):
        if q == high:
            src, dst, hop = pan[0][0].at[s, part_of(h, high)], pan[q][h].at[s], q
        elif q > high:
            src, dst, hop = pan[high][h].at[s], pan[q][0].at[s, part_of(h, high)], q - high
        else:
            src, dst, hop = pan[0][0].at[s, part_of(h, high)], pan[q][0].at[s, part_of(h, high)], q
        return pltpu.make_async_remote_copy(
            src_ref=src, dst_ref=dst, send_sem=z_send.at[q - 1, h], recv_sem=z_recv.at[q - 1, h],
            device_id={"op": op_at(hop)}, device_id_type=MESH)

    def s_copy(q, h, d, block):
        return pltpu.make_async_remote_copy(
            src_ref=pan[q][h].at[block], dst_ref=pan[q][h].at[block], send_sem=s_send.at[q, h, d - 1],
            recv_sem=s_recv.at[q, h, d - 1], device_id={"sec": ((g + d) % groups) * 2 + core}, device_id_type=MESH)

    def m_copy(q, h, d, block):
        return pltpu.make_async_remote_copy(
            src_ref=pan[q][h].at[block], dst_ref=pan[q][h].at[block], send_sem=m_send.at[q, h, d],
            recv_sem=m_recv.at[q, h, d], device_id={"sec": mate}, device_id_type=MESH)

    def x_copy(q, h, c):
        part = (pl.ds(c * per, per), part_of(h, q))
        return pltpu.make_async_remote_copy(
            src_ref=xs.at[(q - 1, *part)], dst_ref=xr.at[(q, *part)], send_sem=x_send.at[q - 1, h, c],
            recv_sem=x_recv.at[q - 1, h, c], device_id={"op": op_at(q)}, device_id_type=MESH)

    def near_copy(q):
        return pltpu.make_async_remote_copy(
            src_ref=near_out.at[q], dst_ref=near_in.at[q], send_sem=near_send.at[q], recv_sem=near_recv.at[q],
            device_id={"op": op_at(1)}, device_id_type=MESH)

    def far_copy(q, to):
        return pltpu.make_async_remote_copy(
            src_ref=far_out.at[q, to - 1], dst_ref=far_in.at[q, to - 1], send_sem=far_send.at[q, to - 1],
            recv_sem=far_recv.at[q, to - 1], device_id={"op": op_at(to)}, device_id_type=MESH)

    def spread(q, h):
        @pl.loop(1, groups)
        def _(d):
            s_copy(q, h, d, s).start()

        m_copy(q, h, 0, s).start()

    def collect(q, h):
        @pl.loop(1, groups)
        def _(d):
            block = from_group(d) * 2 + core
            s_copy(q, h, d, block).wait_recv()
            m_copy(q, h, d, block).start()

        @pl.loop(0, groups)
        def _(d):
            m_copy(q, h, d, from_group(d) * 2 + 1 - core).wait_recv()

    def images(q, h, c):
        @pl.loop(0, per, unroll=True)
        def _(i):
            k = c * per + i
            image = lax.dot_general(
                pan[q][h][src_ref[0, k]], rv[k], (((1,), (1,)), ((), ())), preferred_element_type=jnp.float32)
            image = jnp.where(k < cnt_ref[0, 0], image, jnp.zeros_like(image)).astype(jnp.bfloat16)
            if q:
                xs[q - 1, k, part_of(h, q)] = image
            else:
                xr[0, k, part_of(h, q)] = image

    def make(q, h):
        collect(q, h)

        @pl.loop(0, chunks)
        def _(c):
            images(q, h, c)
            if q:
                x_copy(q, h, c).start()

    pieces = range(len(parts[high]))
    for q in [high] + list(range(1, high)):
        for h in pieces:
            z_copy(q, h).start()
    for h in pieces:
        z_copy(high, h).wait_recv()
        spread(high, h)
        for q in range(high + 1, n_op):
            z_copy(q, h).start()
    load_r.wait()
    for h in pieces:
        make(high, h)
    for q in order[1:]:
        for h in pieces:
            z_copy(q, h).wait_recv()
        spread(q, 0)
    spread(0, 0)
    for q in order[1:] + [0]:
        make(q, 0)
    load_l.wait()

    def rows_of(q):
        return pl.ds(pl.multiple_of(op_at(q) * rows, rows), rows)

    def swapped(to):
        return flip(to, 1) - 1

    def gather(q):
        @pl.loop(0, chunks)
        def _(c):
            if q:
                for h in range(len(parts[q])):
                    x_copy(q, h, c).wait_recv()
            lefts = jnp.concatenate([lv[c * per + i] for i in range(per)], axis=1)
            block = xr[q, pl.ds(c * per, per)].reshape(per * rows, width)
            acc[q] += jnp.dot(lefts, block, preferred_element_type=jnp.float32)

    for q in early + late:
        gather(q)
        if q in early:
            for to in range(1, n_op):
                near_out[q, to - 1] = acc[q, rows_of(to), :].astype(near_out.dtype)
            near_copy(q).start()
            continue
        if early:
            near_copy(flip(q, 1)).wait_recv()
        for to in reversed(range(1, n_op)):
            total = acc[q, rows_of(to), :]
            if early and to > 1:
                total = total + near_in[flip(q, 1), swapped(to)].astype(jnp.float32)
            far_out[q, to - 1] = total.astype(far_out.dtype)
            far_copy(q, to).start()

    def cols_of(q):
        return pl.ds(pl.multiple_of(op_at(q) * width, width), width)

    def take(q, to):
        far_copy(flip(q, to), to).wait_recv()
        return far_in[flip(q, to), to - 1].astype(jnp.float32)

    for q in range(n_op):
        total = acc[q, rows_of(0), :]
        if not early:
            for to in range(1, n_op):
                total = total + take(q, to)
        elif q in early:
            total = total + take(q, 1) + take(q, 2)
        else:
            total = total + near_in[flip(q, 1), 0].astype(jnp.float32) + take(q, 3)
        row_ids = j * rows + lax.broadcasted_iota(jnp.int32, (rows, width), 0)
        col_ids = op_at(q) * width + lax.broadcasted_iota(jnp.int32, (rows, width), 1)
        keep = (row_ids < dl_ref[0, 0]) & (col_ids < dr_ref[0, 0])
        out_ref[:, cols_of(q)] = jnp.where(keep, total, jnp.zeros_like(total)).astype(out_ref.dtype)

    for q in range(n_op):
        for h in range(len(parts[q])):
            @pl.loop(1, groups)
            def _(d):
                s_copy(q, h, d, s).wait_send()

            @pl.loop(0, groups)
            def _(d):
                m_copy(q, h, d, s).wait_send()

            if q:
                @pl.loop(0, chunks)
                def _(c):
                    x_copy(q, h, c).wait_send()

        if q in early:
            near_copy(q).wait_send()
        else:
            for to in range(1, n_op):
                far_copy(q, to).wait_send()
        if q:
            for h in pieces:
                z_copy(q, h).wait_send()


def solution(mesh):
    n_sec, n_op = mesh.shape["sec"], mesh.shape["op"]

    def body(psi, left_ops, right_ops, sources, counts, dims_left, dims_right):
        rows, cols = psi.shape[1:]
        terms, _, height, depth = left_ops.shape
        width = right_ops.shape[2]
        groups = n_sec // 2
        chunks = max(c for c in range(1, 3) if terms % c == 0)
        parts = [(rows,)] * n_op
        parts[n_op // 2] = (rows // 4, rows - rows // 4)
        most = max(len(p) for p in parts)
        bf, dma = jnp.bfloat16, pltpu.SemaphoreType.DMA
        vmem, smem = pl.BlockSpec(memory_space=pltpu.VMEM), pl.BlockSpec(memory_space=pltpu.SMEM)
        hbm = pl.BlockSpec(memory_space=pl.ANY)
        out = pl.pallas_call(
            functools.partial(kernel, n_sec, n_op, chunks, parts),
            out_shape=jax.ShapeDtypeStruct((rows, cols), bf),
            in_specs=[hbm, hbm, hbm, smem, smem, smem, smem],
            out_specs=vmem,
            scratch_shapes=[pltpu.VMEM((n_sec, h, cols), bf) for p in parts for h in p] + [
                pltpu.VMEM((rows, cols), bf),
                pltpu.VMEM((terms, height, depth), bf),
                pltpu.VMEM((terms, width, cols), bf),
                pltpu.VMEM((n_op - 1, terms, rows, width), bf),
                pltpu.VMEM((n_op, terms, rows, width), bf),
                pltpu.VMEM((n_op, height, width), jnp.float32),
                dma((3,)),
                dma((n_op - 1, most)), dma((n_op - 1, most)),
                dma((n_op, most, groups - 1)), dma((n_op, most, groups - 1)),
                dma((n_op, most, groups)), dma((n_op, most, groups)),
                dma((n_op - 1, most, chunks)), dma((n_op - 1, most, chunks)),
                pltpu.VMEM((n_op, n_op - 1, rows, width), bf), pltpu.VMEM((n_op, n_op - 1, rows, width), bf),
                pltpu.VMEM((n_op, n_op - 1, rows, width), bf), pltpu.VMEM((n_op, n_op - 1, rows, width), bf),
                dma((n_op,)), dma((n_op,)), dma((n_op, n_op - 1)), dma((n_op, n_op - 1)),
            ],
            compiler_params=pltpu.CompilerParams(
                collective_id=0, has_side_effects=True, vmem_limit_bytes=60 * 2**20),
        )(psi[0], left_ops[:, 0], right_ops[:, 0], sources, counts[None], dims_left[None], dims_right[None])
        return out[None]

    return jax.shard_map(
        body,
        mesh=mesh,
        in_specs=(
            P("sec", "op", None),
            P(None, "sec", None, "op"),
            P(None, "sec", "op", None),
            P("sec", None),
            P("sec"),
            P("sec"),
            P("sec"),
        ),
        out_specs=P("sec", "op", None),
        check_vma=False,
    )
```

```python
import functools

import jax
import jax.numpy as jnp
from jax import lax
from jax.experimental import pallas as pl
from jax.experimental.pallas import tpu as pltpu
from jax.sharding import PartitionSpec as P

MESH = pl.DeviceIdType.MESH


def flip(j, q):
    out, bit = 0, 1
    while bit <= q:
        out = out + ((j // bit + q // bit % 2) % 2) * bit
        bit *= 2
    return out + j // bit * bit


def kernel(n_sec, n_op, chunks, parts, psi_hbm, left_hbm, right_hbm, src_ref, cnt_ref, dl_ref, dr_ref, out_ref,
           *scratch):
    pan, at = [], 0
    for q in range(n_op):
        pan.append(scratch[at:at + len(parts[q])])
        at += len(parts[q])
    (psi_v, lv, rv, xs, xr, acc, local_sem, z_send, z_recv, s_send, s_recv, m_send, m_recv, x_send, x_recv,
     near_out, near_in, far_out, far_in, near_send, near_recv, far_send, far_recv) = scratch[at:]
    s = lax.axis_index("sec")
    j = lax.axis_index("op")
    groups = n_sec // 2
    g, core = s // 2, s % 2
    mate = g * 2 + 1 - core
    rows, cols = psi_v.shape
    terms = lv.shape[0]
    width = rv.shape[1]
    per = terms // chunks
    high = n_op // 2
    order = [high] + list(range(1, high)) + list(range(high + 1, n_op))
    early, late = ((2, 1), (0, 3)) if n_op == 4 else ((), tuple(range(n_op)))

    inner = j // 2 != j % 2
    hold = chunks * 2 // 4

    load_p = pltpu.make_async_copy(psi_hbm, psi_v, local_sem.at[2])
    load_r = pltpu.make_async_copy(right_hbm, rv, local_sem.at[0])
    load_l = pltpu.make_async_copy(left_hbm, lv, local_sem.at[1])

    def op_at(q):
        return flip(j, q)

    def from_group(d):
        return (g - d + groups) % groups

    barrier = pltpu.get_barrier_semaphore()
    for q in range(1, n_op):
        pl.semaphore_signal(barrier, inc=1, device_id={"op": op_at(q)}, device_id_type=MESH)

    @pl.loop(1, groups)
    def _(d):
        pl.semaphore_signal(barrier, inc=1, device_id={"sec": ((g + d) % groups) * 2 + core}, device_id_type=MESH)

    pl.semaphore_signal(barrier, inc=1, device_id={"sec": mate}, device_id_type=MESH)

    load_p.start()
    load_r.start()
    load_l.start()

    def inside():
        row_ids = j * rows + lax.broadcasted_iota(jnp.int32, (rows, cols), 0)
        col_ids = lax.broadcasted_iota(jnp.int32, (rows, cols), 1)
        return (row_ids < dl_ref[0]) & (col_ids < dr_ref[0])

    keep = inside()
    acc[...] = jnp.zeros_like(acc)
    load_p.wait()
    psi = psi_v[...]
    pan[0][0][s] = jnp.where(keep, psi, jnp.zeros_like(psi))

    pl.semaphore_wait(barrier, n_op - 1 + groups)

    def part_of(h, q):
        return pl.ds(sum(parts[q][:h]), parts[q][h])

    def z_copy(q, h):
        if q == high:
            src, dst, hop = pan[0][0].at[s, part_of(h, high)], pan[q][h].at[s], q
        elif q > high:
            src, dst, hop = pan[high][h].at[s], pan[q][0].at[s, part_of(h, high)], q - high
        else:
            src, dst, hop = pan[0][0].at[s, part_of(h, high)], pan[q][0].at[s, part_of(h, high)], q
        return pltpu.make_async_remote_copy(
            src_ref=src, dst_ref=dst, send_sem=z_send.at[q - 1, h], recv_sem=z_recv.at[q - 1, h],
            device_id={"op": op_at(hop)}, device_id_type=MESH)

    def s_copy(q, h, d, block):
        return pltpu.make_async_remote_copy(
            src_ref=pan[q][h].at[block], dst_ref=pan[q][h].at[block], send_sem=s_send.at[q, h, d - 1],
            recv_sem=s_recv.at[q, h, d - 1], device_id={"sec": ((g + d) % groups) * 2 + core}, device_id_type=MESH)

    def m_copy(q, h, d, block):
        return pltpu.make_async_remote_copy(
            src_ref=pan[q][h].at[block], dst_ref=pan[q][h].at[block], send_sem=m_send.at[q, h, d],
            recv_sem=m_recv.at[q, h, d], device_id={"sec": mate}, device_id_type=MESH)

    def x_copy(q, h, c):
        part = (pl.ds(c * per, per), part_of(h, q))
        return pltpu.make_async_remote_copy(
            src_ref=xs.at[(q - 1, *part)], dst_ref=xr.at[(q, *part)], send_sem=x_send.at[q - 1, h, c],
            recv_sem=x_recv.at[q - 1, h, c], device_id={"op": op_at(q)}, device_id_type=MESH)

    def near_copy(q):
        return pltpu.make_async_remote_copy(
            src_ref=near_out.at[q], dst_ref=near_in.at[q], send_sem=near_send.at[q], recv_sem=near_recv.at[q],
            device_id={"op": op_at(1)}, device_id_type=MESH)

    def far_copy(q, to):
        return pltpu.make_async_remote_copy(
            src_ref=far_out.at[q, to - 1], dst_ref=far_in.at[q, to - 1], send_sem=far_send.at[q, to - 1],
            recv_sem=far_recv.at[q, to - 1], device_id={"op": op_at(to)}, device_id_type=MESH)

    def spread(q, h):
        @pl.loop(1, groups)
        def _(d):
            s_copy(q, h, d, s).start()

        m_copy(q, h, 0, s).start()

    def collect(q, h):
        @pl.loop(1, groups)
        def _(d):
            block = from_group(d) * 2 + core
            s_copy(q, h, d, block).wait_recv()
            m_copy(q, h, d, block).start()

        @pl.loop(0, groups)
        def _(d):
            m_copy(q, h, d, from_group(d) * 2 + 1 - core).wait_recv()

    def images(q, h, c):
        @pl.loop(0, per, unroll=True)
        def _(i):
            k = c * per + i
            image = lax.dot_general(
                pan[q][h][src_ref[0, k]], rv[k], (((1,), (1,)), ((), ())), preferred_element_type=jnp.float32)
            image = jnp.where(k < cnt_ref[0], image, jnp.zeros_like(image)).astype(jnp.bfloat16)
            if q:
                xs[q - 1, k, part_of(h, q)] = image
            else:
                xr[0, k, part_of(h, q)] = image

    def make(q, h):
        collect(q, h)

        @pl.loop(0, chunks)
        def _(c):
            images(q, h, c)
            if early and q == late[-1]:
                @pl.when(inner)
                def _():
                    x_copy(q, h, c).start()
            elif q:
                x_copy(q, h, c).start()

    pieces = range(len(parts[high]))
    for q in [high] + list(range(1, high)):
        for h in pieces:
            z_copy(q, h).start()
    for h in pieces:
        z_copy(high, h).wait_recv()
        spread(high, h)
        for q in range(high + 1, n_op):
            z_copy(q, h).start()
    for q in range(1, high):
        for h in pieces:
            z_copy(q, h).wait_recv()
        spread(q, 0)
    load_r.wait()
    for h in pieces:
        make(high, h)
    for q in range(high + 1, n_op):
        for h in pieces:
            z_copy(q, h).wait_recv()
        spread(q, 0)
    spread(0, 0)
    for q in order[1:] + [0]:
        make(q, 0)
    load_l.wait()

    def rows_of(q):
        return pl.ds(pl.multiple_of(op_at(q) * rows, rows), rows)

    def swapped(to):
        return flip(to, 1) - 1

    def gather(q):
        @pl.loop(0, chunks)
        def _(c):
            if q:
                for h in range(len(parts[q])):
                    x_copy(q, h, c).wait_recv()
            lefts = jnp.concatenate([lv[c * per + i] for i in range(per)], axis=1)
            block = xr[q, pl.ds(c * per, per)].reshape(per * rows, width)
            acc[q] += jnp.dot(lefts, block, preferred_element_type=jnp.float32)

    def resume(first, end):
        @pl.when(jnp.logical_not(inner))
        def _():
            @pl.loop(first, end)
            def _(c):
                x_copy(late[-1], 0, c).start()

    for q in early + late:
        if early and q == late[0]:
            resume(0, hold)
        if early and q == late[-1]:
            resume(hold, chunks)
        if q == late[-1]:
            for q in range(n_op):
                for h in range(len(parts[q])):
                    @pl.loop(1, groups)
                    def _(d):
                        s_copy(q, h, d, s).wait_send()

                    @pl.loop(0, groups)
                    def _(d):
                        m_copy(q, h, d, s).wait_send()

                if q:
                    for h in pieces:
                        z_copy(q, h).wait_send()

        gather(q)
        if q in early:
            for to in range(1, n_op):
                near_out[q, to - 1] = acc[q, rows_of(to), :].astype(near_out.dtype)
            near_copy(q).start()
            continue
        if early:
            near_copy(flip(q, 1)).wait_recv()
        for to in reversed(range(1, n_op)):
            total = acc[q, rows_of(to), :]
            if early and to > 1:
                total = total + near_in[flip(q, 1), swapped(to)].astype(jnp.float32)
            far_out[q, to - 1] = total.astype(far_out.dtype)
            far_copy(q, to).start()

    def cols_of(q):
        return pl.ds(pl.multiple_of(op_at(q) * width, width), width)

    def take(q, to):
        far_copy(flip(q, to), to).wait_recv()
        return far_in[flip(q, to), to - 1].astype(jnp.float32)

    for q in range(n_op):
        total = acc[q, rows_of(0), :]
        if not early:
            for to in range(1, n_op):
                total = total + take(q, to)
        elif q in early:
            total = total + take(q, 1) + take(q, 2)
        else:
            total = total + near_in[flip(q, 1), 0].astype(jnp.float32) + take(q, 3)
        row_ids = j * rows + lax.broadcasted_iota(jnp.int32, (rows, width), 0)
        col_ids = op_at(q) * width + lax.broadcasted_iota(jnp.int32, (rows, width), 1)
        keep = (row_ids < dl_ref[0]) & (col_ids < dr_ref[0])
        out_ref[:, cols_of(q)] = jnp.where(keep, total, jnp.zeros_like(total)).astype(out_ref.dtype)

    for q in range(n_op):
        for h in range(len(parts[q])):
            if q:
                @pl.loop(0, chunks)
                def _(c):
                    x_copy(q, h, c).wait_send()

        if q in early:
            near_copy(q).wait_send()
        else:
            for to in range(1, n_op):
                far_copy(q, to).wait_send()

def solution(mesh):
    n_sec, n_op = mesh.shape["sec"], mesh.shape["op"]

    def body(psi, left_ops, right_ops, sources, counts, dims_left, dims_right):
        rows, cols = psi.shape[1:]
        terms, _, height, depth = left_ops.shape
        width = right_ops.shape[2]
        groups = n_sec // 2
        chunks = max(c for c in range(1, 5) if terms % c == 0)
        parts = [(rows,)] * n_op
        parts[n_op // 2] = (rows // 4, rows - rows // 4)
        most = max(len(p) for p in parts)
        bf, dma = jnp.bfloat16, pltpu.SemaphoreType.DMA
        vmem, smem = pl.BlockSpec(memory_space=pltpu.VMEM), pl.BlockSpec(memory_space=pltpu.SMEM)
        hbm = pl.BlockSpec(memory_space=pl.ANY)
        out = pl.pallas_call(
            functools.partial(kernel, n_sec, n_op, chunks, parts),
            out_shape=pltpu.VMEM((rows, cols), bf),
            in_specs=[hbm, hbm, hbm, smem, smem, smem, smem],
            out_specs=vmem,
            scratch_shapes=[pltpu.VMEM((n_sec, h, cols), bf) for p in parts for h in p] + [
                pltpu.VMEM((rows, cols), bf),
                pltpu.VMEM((terms, height, depth), bf),
                pltpu.VMEM((terms, width, cols), bf),
                pltpu.VMEM((n_op - 1, terms, rows, width), bf),
                pltpu.VMEM((n_op, terms, rows, width), bf),
                pltpu.VMEM((n_op, height, width), jnp.float32),
                dma((3,)),
                dma((n_op - 1, most)), dma((n_op - 1, most)),
                dma((n_op, most, groups - 1)), dma((n_op, most, groups - 1)),
                dma((n_op, most, groups)), dma((n_op, most, groups)),
                dma((n_op - 1, most, chunks)), dma((n_op - 1, most, chunks)),
                pltpu.VMEM((n_op, n_op - 1, rows, width), bf), pltpu.VMEM((n_op, n_op - 1, rows, width), bf),
                pltpu.VMEM((n_op, n_op - 1, rows, width), bf), pltpu.VMEM((n_op, n_op - 1, rows, width), bf),
                dma((n_op,)), dma((n_op,)), dma((n_op, n_op - 1)), dma((n_op, n_op - 1)),
            ],
            compiler_params=pltpu.CompilerParams(
                collective_id=0, has_side_effects=True, vmem_limit_bytes=60 * 2**20),
        )(psi[0], left_ops[:, 0], right_ops[:, 0], sources, counts, dims_left, dims_right)
        return out[None]

    return jax.shard_map(
        body,
        mesh=mesh,
        in_specs=(
            P("sec", "op", None),
            P(None, "sec", None, "op"),
            P(None, "sec", "op", None),
            P("sec", None),
            P("sec"),
            P("sec"),
            P("sec"),
        ),
        out_specs=P("sec", "op", None),
        check_vma=False,
    )
```
